32 devices in a mesh: ka: 16 (over z, x, core), mu: 2 (over y).
Axes of the slice: x: 2, y: 2, z: 4, core: 2. Of those that a mesh axis runs over, the one named last changes fastest.
Arguments:
- vectors: float32 [3, 16, 4096], P(None, 'ka', 'mu'), may hold values from -6 to 6
- phi_val: bfloat16 [16, 64, 2048], P('ka', None, 'mu'), may hold values from -6 to 6
- phi_con: bfloat16 [16, 64, 2048], P('ka', None, 'mu'), may hold values from -6 to 6
- screened: bfloat16 [4, 2048, 2048], P(None, 'mu'), may hold values from -4.5776367e-05 to 4.5776367e-05
- partner: int32 [16, 4], P('ka'), may hold values from 0 to 15, as said below
Outputs:
- result: float32 [3, 16, 4096], P(None, 'ka', 'mu')
The draws below stay inside these ranges and needn't reach their ends.
Inputs may be any that keep to these rules, and one draw needn't show every extreme that they name: With s = (1, -1, 2, -2) for offsets 0 to 3, partner[k, o] = (k - s[o]) modulo 16; each ka index j holds exactly one k-point, k-point j.
All inputs are finite; a program needn't handle non-finite values.
Results may differ from the reference program's by a relative error of at most 0.0058.
Values may be sent and summed in bfloat16 or wider, within the bound.
No kernel may reach another device: no remote copies, remote signals or barrier semaphores. Data moves between devices by JAX's collectives and lax.ppermute only.
A program may use at most 64 MiB of HBM per device.

```python
import jax
import jax.numpy as jnp
from jax import lax

NV = 64
NC = 64
NMU = 2048
NVEC = 3
NOFF = 4
KD = 1
NK = 16
PAIRS = 4096


cycle_steps = (1, -1, 2, -2)


def draw_partner(key, part):
    blocks = NK // KD
    key_list = jax.random.split(key, blocks * NOFF)
    slot_table = jax.vmap(lambda single: jax.random.permutation(single, KD))(key_list)
    slot_table = jnp.transpose(slot_table.reshape(blocks, NOFF, KD), (0, 2, 1)).astype(jnp.int32)
    home_block = jnp.arange(blocks, dtype=jnp.int32)[:, None, None]
    cycle_shift = jnp.array(cycle_steps, jnp.int32)[None, None, :]
    source = jnp.mod(home_block - cycle_shift, blocks)
    return (source * KD + slot_table).reshape(NK, NOFF)


def block_scale(own_key, dims, cuts, low, largest):
    def one(dim, shards_of):
        steps = jax.random.uniform(jax.random.fold_in(jax.random.fold_in(own_key, 6), dim), (shards_of,), jnp.float32, low / len(cuts), largest / len(cuts))
        return jnp.repeat(jnp.exp(steps), dims[dim] // shards_of).reshape((-1,) + (1,) * (len(dims) - dim - 1))

    factor_of = one(*cuts[0])
    for cut in cuts[1:]:
        factor_of = factor_of * one(*cut)
    return factor_of


def centred(rng, shape, spread, reach, pieces=(), kind=jnp.bfloat16):
    factor_of = block_scale(rng, shape, pieces, -0.22, 0.18) if pieces else 1.0
    values = jax.random.normal(rng, shape, jnp.float32) * spread * factor_of
    return jnp.minimum(jnp.maximum(values, -reach), reach).astype(kind)


def setup_inputs(seed: int = 0) -> dict:
    splits = jax.random.split(jax.random.key(seed), 6)
    vectors = centred(splits[0], (NVEC, NK, PAIRS), 1.0, 6.0, ((1, 16), (2, 2)), jnp.float32)
    phi_val = centred(splits[1], (NK, NV, NMU), 1.0, 6.0, ((0, 16), (2, 2)))
    phi_con = centred(splits[2], (NK, NC, NMU), 1.0, 6.0, ((0, 16), (2, 2)))
    screened = centred(splits[3], (NOFF, NMU, NMU), (1.0 / (NMU * NV)), 4.57763671875e-05, ((1, 2),))
    partner = draw_partner(jax.random.fold_in(splits[5], 71), 0)
    return {"vectors": vectors, "phi_val": phi_val, "phi_con": phi_con, "screened": screened, "partner": partner}


def reference(vectors, phi_val, phi_con, screened, partner):
    vec_coded = vectors.astype(jnp.bfloat16).reshape(NVEC, NK, NV, NC)

    def one_point(point_item):
        val_own, con_own, partners = point_item
        running_sum = jnp.zeros((NVEC, NV, NC), jnp.float32)
        for offset in range(NOFF):
            source = partners[offset]
            val_far = lax.dynamic_index_in_dim(phi_val, source, 0, keepdims=False)
            con_far = lax.dynamic_index_in_dim(phi_con, source, 0, keepdims=False)
            vec_far = lax.dynamic_index_in_dim(vec_coded, source, 1, keepdims=False)
            blended = jnp.einsum('svc,cn->svn', vec_far.astype(jnp.float32), con_far.astype(jnp.float32)).astype(jnp.bfloat16)
            paired = jnp.einsum('vm,svn->smn', val_far.astype(jnp.float32), blended.astype(jnp.float32))
            weighted = (screened[offset].astype(jnp.float32)[None] * paired).astype(jnp.bfloat16)
            folded = jnp.einsum('smn,cn->smc', weighted.astype(jnp.float32), con_own.astype(jnp.float32)).astype(jnp.bfloat16)
            running_sum = running_sum + jnp.einsum('vm,smc->svc', val_own.astype(jnp.float32), folded.astype(jnp.float32))
        return running_sum

    gathered = lax.map(one_point, (phi_val, phi_con, partner))
    return jnp.transpose(gathered, (1, 0, 2, 3)).reshape(NVEC, NK, NV * NC)
```

```python
import functools

import jax
import jax.numpy as jnp
from jax import lax
from jax.experimental import pallas as pl
from jax.experimental.pallas import tpu as pltpu
from jax.sharding import PartitionSpec as P

BF16, F32 = jnp.bfloat16, jnp.float32
VMEM_SPEC = pl.BlockSpec(memory_space=pltpu.VMEM)
SMEM_SPEC = pl.BlockSpec(memory_space=pltpu.SMEM)
HBM_SPEC = pl.BlockSpec(memory_space=pl.ANY)
MIB = 1 << 20
NEAR, FAR, AHEAD, BEHIND = range(4)


def contract(left, right, left_dim, right_dim):
    dims = (((left_dim,), (right_dim,)), ((), ()))
    return lax.dot_general(left, right, dims, preferred_element_type=F32)


def screened_copy(screened, info, slot, part, cols, buffer, sem):
    count = screened.shape[2] // cols
    home = lax.rem(info[0] + part, count)
    columns = pl.ds(pl.multiple_of(home * cols, cols), cols)
    return pltpu.make_async_copy(
        screened.at[info[1 + slot], :, columns], buffer.at[:, pl.ds(part * cols, cols)], sem
    )


def first_kernel(count, info, *refs):
    vec_parts, con_parts = refs[:count], refs[count : 2 * count]
    val_home, val_near, screened, pairs, folded, vec_all, buffer, sems = refs[2 * count :]
    vec_count, rows, conduction = vec_parts[0].shape
    cols = con_parts[0].shape[1]
    for part in range(count):
        screened_copy(screened, info, NEAR, part, cols, buffer, sems.at[part]).start()
    for part in range(count):
        offset = pl.multiple_of(lax.rem(info[0] + part, count) * rows, rows)
        for s in range(vec_count):
            vec_all[s, pl.ds(offset, rows), :] = vec_parts[part][s].astype(F32)
    for s in range(vec_count):
        half = contract(val_home[...], vec_all[s].astype(BF16), 0, 0).astype(BF16)
        for part in range(count):
            pairs[s, :, pl.ds(part * cols, cols)] = contract(
                half, con_parts[part][...], 1, 0
            ).astype(BF16)
    for part in range(count):
        screened_copy(screened, info, NEAR, part, cols, buffer, sems.at[part]).wait()
    valence = val_near.shape[0]
    for s in range(vec_count):
        folded[pl.ds(s * valence, valence), :] = contract(
            val_near[...], buffer[...] * pairs[s], 1, 0
        ).astype(BF16)


def fold_kernel(count, slots, info, *refs):
    used = len(slots)
    pairs, screened = refs[:2]
    vals, foldeds = refs[2 : 2 + used], refs[3 + used : 3 + 2 * used]
    buffers, sems = refs[-2:]
    vec_count, _, points = pairs.shape
    cols = points // count
    valence = vals[0].shape[0]
    for i, slot in enumerate(slots):
        for part in range(count):
            screened_copy(screened, info, slot, part, cols, buffers.at[i], sems.at[i, part]).start()
    for i, slot in enumerate(slots):
        for part in range(count):
            screened_copy(screened, info, slot, part, cols, buffers.at[i], sems.at[i, part]).wait()
        for s in range(vec_count):
            foldeds[i][pl.ds(s * valence, valence), :] = contract(
                vals[i][...], buffers[i] * pairs[s], 1, 0
            ).astype(BF16)


def result_kernel(count, used, info, *refs):
    foldeds, cons = refs[:used], refs[used : used + used * count]
    outs, work = refs[used + used * count : -1], refs[-1]
    vec_count, rows, _ = outs[0].shape
    valence = foldeds[0].shape[0] // vec_count
    cols = cons[0].shape[1]
    for i in range(used):
        total = contract(foldeds[i][:, pl.ds(0, cols)], cons[i * count][...], 1, 1)
        for part in range(1, count):
            total += contract(
                foldeds[i][:, pl.ds(part * cols, cols)], cons[i * count + part][...], 1, 1
            )
        work[i] = total
        for part in range(count):
            offset = lax.rem(info[0] + part, count) * rows
            for s in range(vec_count):
                start = pl.multiple_of(s * valence + offset, 8)
                outs[i * count + part][s] = work[i, pl.ds(start, rows), :]


def moved(value, pairs_of):
    ka, mu = lax.axis_size("ka"), lax.axis_size("mu")
    pairs = []
    for k in range(ka):
        for m in range(mu):
            k_to, m_to = pairs_of(k, m)
            pairs.append((k * mu + m, (k_to % ka) * mu + m_to % mu))
    return lax.ppermute(value, ("ka", "mu"), pairs)


def target_of(slot, k):
    sign = 1 - 2 * (k % 2)
    return k + sign * {NEAR: 1, FAR: -1, AHEAD: 2, BEHIND: -2}[slot]


def local(vectors, phi_val, phi_con, screened, partner):
    del partner
    ka, count = lax.axis_size("ka"), lax.axis_size("mu")
    vec_count, local_k, local_pairs = vectors.shape
    _, valence, rows_m = phi_val.shape
    _, conduction, cols = phi_con.shape
    points = screened.shape[2]
    if local_k != 1 or ka % 2:
        raise ValueError("unsupported shapes")
    rows = local_pairs // conduction

    me, parity = lax.axis_index("mu"), lax.axis_index("ka") % 2
    info = jnp.concatenate([me[None], jnp.arange(4) ^ parity]).astype(jnp.int32)

    def from_slot(slot):
        back = {NEAR: NEAR, FAR: FAR, AHEAD: BEHIND, BEHIND: AHEAD}[slot]
        if slot in (AHEAD, BEHIND):
            return lambda k, m: (target_of(back, k), m)
        return lambda k, m: (target_of(slot, k), m)

    def over_mu(value):
        return [value] + [
            moved(value, lambda k, m, t=t: (k, m - t)) for t in range(1, count)
        ]

    val_home, con_home = phi_val[0], phi_con[0]
    vec_home = vectors.astype(BF16).reshape(vec_count, rows, conduction)
    vec_parts = over_mu(vec_home)
    con_parts = over_mu(con_home)
    val = {s: moved(val_home, from_slot(s)) for s in (NEAR, AHEAD, BEHIND)}
    con = {s: moved(con_home, from_slot(s)) for s in (AHEAD, BEHIND)}
    val[FAR] = moved(val[AHEAD], from_slot(NEAR))
    con_all = {s: over_mu(con[s]) for s in (AHEAD, BEHIND)}
    con_all[NEAR] = [moved(part, from_slot(NEAR)) for part in con_parts]
    con_all[FAR] = [moved(part, from_slot(NEAR)) for part in con_all[AHEAD]]

    pairs_type = jax.ShapeDtypeStruct((vec_count, rows_m, points), BF16)
    folded_type = jax.ShapeDtypeStruct((vec_count * valence, points), BF16)
    result_type = jax.ShapeDtypeStruct((vec_count, rows, conduction), F32)
    fold_flops = 2 * vec_count * valence * rows_m * points

    def params(mib):
        return pltpu.CompilerParams(vmem_limit_bytes=mib * MIB)

    pairs, folded_near = pl.pallas_call(
        functools.partial(first_kernel, count),
        out_shape=[pairs_type, folded_type],
        in_specs=[SMEM_SPEC] + [VMEM_SPEC] * (2 * count + 2) + [HBM_SPEC],
        out_specs=[VMEM_SPEC] * 2,
        scratch_shapes=[
            pltpu.VMEM((vec_count, valence, conduction), F32),
            pltpu.VMEM((rows_m, points), BF16),
            pltpu.SemaphoreType.DMA((count,)),
        ],
        compiler_params=params(30),
        cost_estimate=pl.CostEstimate(flops=8 * fold_flops, bytes_accessed=4 * MIB, transcendentals=0),
        name="first",
    )(info, *vec_parts, *con_parts, val_home, val[NEAR], screened)

    def fold(pairs, *slots):
        used = len(slots)
        out = pl.pallas_call(
            functools.partial(fold_kernel, count, slots),
            out_shape=[pairs_type] + [folded_type] * used,
            in_specs=[SMEM_SPEC, VMEM_SPEC, HBM_SPEC] + [VMEM_SPEC] * used,
            out_specs=[VMEM_SPEC] * (1 + used),
            scratch_shapes=[
                pltpu.VMEM((used, rows_m, points), BF16),
                pltpu.SemaphoreType.DMA((used, count)),
            ],
            input_output_aliases={1: 0},
            compiler_params=params(30),
            cost_estimate=pl.CostEstimate(
                flops=4 * used * fold_flops, bytes_accessed=4 * used * MIB, transcendentals=0
            ),
            name="fold%d" % used,
        )(info, pairs, screened, *[val[s] for s in slots])
        return out[0], out[1:]

    def results(foldeds, *slots):
        used = len(slots)
        out = pl.pallas_call(
            functools.partial(result_kernel, count, used),
            out_shape=[result_type] * (used * count),
            in_specs=[SMEM_SPEC] + [VMEM_SPEC] * (used + used * count),
            out_specs=[VMEM_SPEC] * (used * count),
            scratch_shapes=[pltpu.VMEM((used, vec_count * valence, conduction), F32)],
            compiler_params=params(10),
            cost_estimate=pl.CostEstimate(
                flops=2 * used * fold_flops // 8, bytes_accessed=MIB, transcendentals=0
            ),
            name="result%d" % used,
        )(info, *foldeds, *[part for s in slots for part in con_all[s]])
        received = []
        for i, slot in enumerate(slots):
            for part in range(count):
                received.append(
                    moved(
                        out[i * count + part],
                        lambda k, m, slot=slot, part=part: (target_of(slot, k), m + part),
                    )
                )
        return received

    pairs, (folded_ahead, folded_behind) = fold(pairs, AHEAD, BEHIND)
    received = results((folded_near, folded_ahead, folded_behind), NEAR, AHEAD, BEHIND)
    pairs, (folded_far,) = fold(pairs, FAR)
    received += results((folded_far,), FAR)
    total = functools.reduce(jnp.add, received)
    return total.reshape(vec_count, 1, local_pairs)


def solution(mesh):
    placed = (
        P(None, "ka", "mu"),
        P("ka", None, "mu"),
        P("ka", None, "mu"),
        P(None, "mu", None),
        P("ka", None),
    )
    return jax.shard_map(
        local, mesh=mesh, in_specs=placed, out_specs=P(None, "ka", "mu"), check_vma=False
    )
```

```python
import functools

import jax
import jax.numpy as jnp
from jax import lax
from jax.experimental import pallas as pl
from jax.experimental.pallas import tpu as pltpu
from jax.sharding import PartitionSpec as P

BF16, F32 = jnp.bfloat16, jnp.float32
VMEM_SPEC = pl.BlockSpec(memory_space=pltpu.VMEM)
SMEM_SPEC = pl.BlockSpec(memory_space=pltpu.SMEM)
HBM_SPEC = pl.BlockSpec(memory_space=pltpu.HBM)
MIB = 1 << 20
NEAR, FAR, AHEAD, BEHIND = range(4)


def contract(left, right, left_dim, right_dim):
    dims = (((left_dim,), (right_dim,)), ((), ()))
    return lax.dot_general(left, right, dims, preferred_element_type=F32)


def screened_copy(screened, info, slot, part, cols, buffer, sem):
    count = screened.shape[2] // cols
    home = lax.rem(info[0] + part, count)
    columns = pl.ds(pl.multiple_of(home * cols, cols), cols)
    return pltpu.make_async_copy(
        screened.at[info[1 + slot], :, columns], buffer.at[:, pl.ds(part * cols, cols)], sem
    )


def first_kernel(count, later, info, *refs):
    vec_parts, con_parts = refs[:count], refs[count : 2 * count]
    bundle_home, bundle_near, screened = refs[2 * count : 2 * count + 3]
    pairs, folded = refs[2 * count + 3 : 2 * count + 5]
    weights = refs[2 * count + 5 : -3]
    vec_all, buffer, sems = refs[-3:]
    vec_count, rows, _ = vec_parts[0].shape
    cols = con_parts[0].shape[1]
    valence = vec_all.shape[1]
    slots, buffers = (NEAR,) + later, (buffer,) + tuple(weights)

    def copies(i):
        return [
            screened_copy(screened, info, slots[i], part, cols, buffers[i], sems.at[i, part])
            for part in range(count)
        ]

    for i in range(len(slots)):
        for copy in copies(i):
            copy.start()
    for part in range(count):
        offset = pl.multiple_of(lax.rem(info[0] + part, count) * rows, rows)
        for s in range(vec_count):
            vec_all[s, pl.ds(offset, rows), :] = vec_parts[part][s].astype(F32)
    for s in range(vec_count):
        half = contract(bundle_home[pl.ds(0, valence), :], vec_all[s].astype(BF16), 0, 0).astype(BF16)
        for part in range(count):
            pairs[s, :, pl.ds(part * cols, cols)] = contract(
                half, con_parts[part][...], 1, 0
            ).astype(BF16)
    for copy in copies(0):
        copy.wait()
    for s in range(vec_count):
        folded[pl.ds(s * valence, valence), :] = contract(
            bundle_near[pl.ds(0, valence), :], buffer[...] * pairs[s], 1, 0
        ).astype(BF16)
    for i in range(1, len(slots)):
        for copy in copies(i):
            copy.wait()


def fold_kernel(count, used, later, info, *refs):
    pairs = refs[0]
    bundles, weights = refs[1 : 1 + used], refs[1 + used : 1 + 2 * used]
    outs = refs[1 + 2 * used :]
    if later:
        screened, outs = outs[0], outs[2:-1]
    foldeds, nexts = outs[:used], outs[used:]
    vec_count, _, points = pairs.shape
    cols = points // count
    valence = foldeds[0].shape[0] // vec_count

    def copies(i):
        return [
            screened_copy(screened, info, later[i], part, cols, nexts[i], refs[-1].at[i, part])
            for part in range(count)
        ]

    for i in range(len(later)):
        for copy in copies(i):
            copy.start()
    for i in range(used):
        for s in range(vec_count):
            foldeds[i][pl.ds(s * valence, valence), :] = contract(
                bundles[i][pl.ds(0, valence), :], weights[i][...] * pairs[s], 1, 0
            ).astype(BF16)
    for i in range(len(later)):
        for copy in copies(i):
            copy.wait()


def result_kernel(count, info, *refs):
    foldeds, bundles = refs[:4], refs[4:8]
    others = refs[8 : 8 + 4 * (count - 1)]
    near, ahead, behind, work = refs[-4:]
    outs = (near.at[0], near.at[1], ahead, behind)
    _, vec_count, rows, _ = ahead.shape
    valence = foldeds[0].shape[0] // vec_count
    cols = bundles[0].shape[1]
    for i in range(4):
        total = contract(
            foldeds[i][:, pl.ds(0, cols)], bundles[i][pl.ds(valence, bundles[i].shape[0] - valence), :], 1, 1
        )
        for part in range(1, count):
            total += contract(
                foldeds[i][:, pl.ds(part * cols, cols)],
                others[i * (count - 1) + part - 1][...],
                1,
                1,
            )
        work[i] = total
        for part in range(count):
            offset = lax.rem(info[0] + part, count) * rows
            for s in range(vec_count):
                start = pl.multiple_of(s * valence + offset, 8)
                outs[i][part, s] = work[i, pl.ds(start, rows), :]


def moved(value, pairs_of):
    ka, mu = lax.axis_size("ka"), lax.axis_size("mu")
    pairs = []
    for k in range(ka):
        for m in range(mu):
            k_to, m_to = pairs_of(k, m)
            pairs.append((k * mu + m, (k_to % ka) * mu + m_to % mu))
    return lax.ppermute(value, ("ka", "mu"), pairs)


def target_of(slot, k):
    sign = 1 - 2 * (k % 2)
    return k + sign * {NEAR: 1, FAR: -1, AHEAD: 2, BEHIND: -2}[slot]


def local(vectors, phi_val, phi_con, screened, partner):
    del partner
    ka, count = lax.axis_size("ka"), lax.axis_size("mu")
    vec_count, local_k, local_pairs = vectors.shape
    _, valence, rows_m = phi_val.shape
    _, conduction, _ = phi_con.shape
    points = screened.shape[2]
    if local_k != 1 or ka % 2:
        raise ValueError("unsupported shapes")
    rows = local_pairs // conduction

    me, parity = lax.axis_index("mu"), lax.axis_index("ka") % 2
    info = jnp.concatenate([me[None], jnp.arange(4) ^ parity]).astype(jnp.int32)

    def from_slot(slot):
        back = {NEAR: NEAR, FAR: FAR, AHEAD: BEHIND, BEHIND: AHEAD}[slot]
        if slot in (AHEAD, BEHIND):
            return lambda k, m: (target_of(back, k), m)
        return lambda k, m: (target_of(slot, k), m)

    def over_mu(value):
        return [value] + [moved(value, lambda k, m, t=t: (k, m - t)) for t in range(1, count)]

    con_home = phi_con[0]
    bundle_home = jnp.concatenate([phi_val[0], con_home], axis=0)
    vec_home = vectors.astype(BF16).reshape(vec_count, rows, conduction)
    vec_home, bundle_home, con_home = lax.optimization_barrier((vec_home, bundle_home, con_home))
    vec_parts = over_mu(vec_home)
    con_parts = over_mu(con_home)
    bundle = {s: moved(bundle_home, from_slot(s)) for s in (NEAR, AHEAD, BEHIND)}
    bundle[FAR] = moved(bundle[AHEAD], from_slot(NEAR))
    others = {s: over_mu(bundle[s][valence:])[1:] for s in (AHEAD, BEHIND)}
    others[NEAR] = [moved(part, from_slot(NEAR)) for part in con_parts[1:]]
    others[FAR] = [moved(part, from_slot(NEAR)) for part in others[AHEAD]]

    pairs_type = jax.ShapeDtypeStruct((vec_count, rows_m, points), BF16)
    folded_type = jax.ShapeDtypeStruct((vec_count * valence, points), BF16)
    weight_type = jax.ShapeDtypeStruct((rows_m, points), BF16)
    fold_flops = 2 * vec_count * valence * rows_m * points

    def params(mib):
        return pltpu.CompilerParams(vmem_limit_bytes=mib * MIB)

    later = (AHEAD, BEHIND)
    first = pl.pallas_call(
        functools.partial(first_kernel, count, later),
        out_shape=[pairs_type, folded_type] + [weight_type] * len(later),
        in_specs=[SMEM_SPEC] + [VMEM_SPEC] * (2 * count + 2) + [HBM_SPEC],
        out_specs=[VMEM_SPEC] * (2 + len(later)),
        scratch_shapes=[
            pltpu.VMEM((vec_count, valence, conduction), F32),
            pltpu.VMEM((rows_m, points), BF16),
            pltpu.SemaphoreType.DMA((1 + len(later), count)),
        ],
        compiler_params=params(24),
        cost_estimate=pl.CostEstimate(flops=8 * fold_flops, bytes_accessed=4 * MIB, transcendentals=0),
        name="first",
    )
    pairs, folded_near, *weights = first(
        info, *vec_parts, *con_parts, bundle_home, bundle[NEAR], screened
    )

    def fold(pairs, weights, slots, later):
        used = len(slots)
        extra = len(later)
        out = pl.pallas_call(
            functools.partial(fold_kernel, count, used, later),
            out_shape=[pairs_type] * bool(extra)
            + [folded_type] * used
            + [weight_type] * extra,
            in_specs=[SMEM_SPEC]
            + [VMEM_SPEC] * (1 + 2 * used)
            + [HBM_SPEC] * bool(extra),
            out_specs=[VMEM_SPEC] * (bool(extra) + used + extra),
            scratch_shapes=[pltpu.SemaphoreType.DMA((extra, count))] * bool(extra),
            input_output_aliases={1: 0} if extra else {},
            compiler_params=params(20),
            cost_estimate=pl.CostEstimate(
                flops=4 * used * fold_flops, bytes_accessed=4 * used * MIB, transcendentals=0
            ),
        )(info, pairs, *[bundle[s] for s in slots], *weights, *[screened] * bool(extra))
        if extra:
            pairs, out = out[0], out[1:]
        return pairs, out[:used], out[used:]

    pairs, (folded_ahead, folded_behind), weights = fold(pairs, weights, (AHEAD, BEHIND), (FAR,))
    _, (folded_far,), _ = fold(pairs, weights, (FAR,), ())

    result = (count, vec_count, rows, conduction)
    order = (NEAR, FAR, AHEAD, BEHIND)
    near, ahead, behind = pl.pallas_call(
        functools.partial(result_kernel, count),
        out_shape=[jax.ShapeDtypeStruct(s, F32) for s in ((2,) + result, result, result)],
        in_specs=[SMEM_SPEC] + [VMEM_SPEC] * (4 + 4 * count),
        out_specs=[VMEM_SPEC] * 3,
        scratch_shapes=[pltpu.VMEM((4, vec_count * valence, conduction), F32)],
        compiler_params=params(10),
        cost_estimate=pl.CostEstimate(flops=fold_flops, bytes_accessed=MIB, transcendentals=0),
        name="result",
    )(
        info,
        folded_near,
        folded_far,
        folded_ahead,
        folded_behind,
        *[bundle[s] for s in order],
        *[part for s in order for part in others[s]],
    )
    near = moved(near, lambda k, m: (target_of(NEAR, k), m))
    shared = jnp.stack([near[0], ahead + near[1], behind])
    summed = shared[:, 0]
    for part in range(1, count):
        summed += moved(shared[:, part], lambda k, m, part=part: (k, m + part))
    total = summed[0]
    for i, slot in ((1, AHEAD), (2, BEHIND)):
        total += moved(summed[i], lambda k, m, slot=slot: (target_of(slot, k), m))
    return total.reshape(vec_count, 1, local_pairs)


def solution(mesh):
    placed = (
        P(None, "ka", "mu"),
        P("ka", None, "mu"),
        P("ka", None, "mu"),
        P(None, "mu", None),
        P("ka", None),
    )

    return jax.shard_map(
        local, mesh=mesh, in_specs=placed, out_specs=P(None, "ka", "mu"), check_vma=False
    )
```

```python
import functools

import jax
import jax.numpy as jnp
from jax import lax
from jax.experimental import pallas as pl
from jax.experimental.pallas import tpu as pltpu
from jax.sharding import PartitionSpec as P

BF16, F32 = jnp.bfloat16, jnp.float32
VMEM_SPEC = pl.BlockSpec(memory_space=pltpu.VMEM)
SMEM_SPEC = pl.BlockSpec(memory_space=pltpu.SMEM)
HBM_SPEC = pl.BlockSpec(memory_space=pltpu.HBM)
MIB = 1 << 20
NEAR, FAR, AHEAD, BEHIND = range(4)


def contract(left, right, left_dim, right_dim):
    dims = (((left_dim,), (right_dim,)), ((), ()))
    return lax.dot_general(left, right, dims, preferred_element_type=F32)


def screened_copy(screened, info, slot, part, cols, buffer, sem):
    count = screened.shape[2] // cols
    home = lax.rem(info[0] + part, count)
    columns = pl.ds(pl.multiple_of(home * cols, cols), cols)
    return pltpu.make_async_copy(
        screened.at[info[1 + slot], :, columns], buffer.at[:, pl.ds(part * cols, cols)], sem
    )


def first_kernel(count, later, info, *refs):
    vec_parts, con_others = refs[:count], refs[count : 2 * count - 1]
    bundle_home, bundle_near, screened = refs[2 * count - 1 : 2 * count + 2]
    pairs, folded = refs[2 * count + 2 : 2 * count + 4]
    weights = refs[2 * count + 4 : -3]
    vec_all, buffer, sems = refs[-3:]
    vec_count, rows, _ = vec_parts[0].shape
    cols = bundle_home.shape[1]
    _, valence, conduction = vec_all.shape
    slots, buffers = (NEAR,) + later, (buffer,) + tuple(weights)

    def copies(i):
        return [
            screened_copy(screened, info, slots[i], part, cols, buffers[i], sems.at[i, part])
            for part in range(count)
        ]

    for i in range(len(slots)):
        for copy in copies(i):
            copy.start()
    for part in range(count):
        offset = pl.multiple_of(lax.rem(info[0] + part, count) * rows, rows)
        for s in range(vec_count):
            vec_all[s, pl.ds(offset, rows), :] = vec_parts[part][s].astype(F32)
    val_points = jnp.transpose(bundle_home[pl.ds(0, valence), :])
    for s in range(vec_count):
        vec = vec_all[s].astype(BF16)
        for part in range(count):
            con = con_others[part - 1][...] if part else bundle_home[pl.ds(valence, conduction), :]
            blended = contract(vec, con, 1, 0).astype(BF16)
            pairs[s, :, pl.ds(part * cols, cols)] = contract(val_points, blended, 1, 0).astype(BF16)
    for copy in copies(0):
        copy.wait()
    for s in range(vec_count):
        folded[pl.ds(s * valence, valence), :] = contract(
            bundle_near[pl.ds(0, valence), :], buffer[...] * pairs[s], 1, 0
        ).astype(BF16)
    for i in range(1, len(slots)):
        for copy in copies(i):
            copy.wait()


def fold_kernel(count, used, later, info, *refs):
    pairs = refs[0]
    bundles, weights = refs[1 : 1 + used], refs[1 + used : 1 + 2 * used]
    outs = refs[1 + 2 * used :]
    if later:
        screened, outs = outs[0], outs[2:-1]
    foldeds, nexts = outs[:used], outs[used:]
    vec_count, _, points = pairs.shape
    cols = points // count
    valence = foldeds[0].shape[0] // vec_count

    def copies(i):
        return [
            screened_copy(screened, info, later[i], part, cols, nexts[i], refs[-1].at[i, part])
            for part in range(count)
        ]

    for i in range(len(later)):
        for copy in copies(i):
            copy.start()
    for i in range(used):
        for s in range(vec_count):
            foldeds[i][pl.ds(s * valence, valence), :] = contract(
                bundles[i][pl.ds(0, valence), :], weights[i][...] * pairs[s], 1, 0
            ).astype(BF16)
    for i in range(len(later)):
        for copy in copies(i):
            copy.wait()


def result_kernel(count, info, *refs):
    foldeds, bundles = refs[:4], refs[4:8]
    others = refs[8 : 8 + 4 * (count - 1)]
    near, far, behind, work = refs[-4:]
    outs = (near.at[0], far, near.at[1], behind)
    _, vec_count, rows, _ = far.shape
    valence = foldeds[0].shape[0] // vec_count
    cols = bundles[0].shape[1]
    for i in range(4):
        total = contract(
            foldeds[i][:, pl.ds(0, cols)], bundles[i][pl.ds(valence, bundles[i].shape[0] - valence), :], 1, 1
        )
        for part in range(1, count):
            total += contract(
                foldeds[i][:, pl.ds(part * cols, cols)],
                others[i * (count - 1) + part - 1][...],
                1,
                1,
            )
        work[i] = total
        for part in range(count):
            offset = lax.rem(info[0] + part, count) * rows
            for s in range(vec_count):
                start = pl.multiple_of(s * valence + offset, 8)
                outs[i][part, s] = work[i, pl.ds(start, rows), :]


def moved(value, pairs_of):
    ka, mu = lax.axis_size("ka"), lax.axis_size("mu")
    pairs = []
    for k in range(ka):
        for m in range(mu):
            k_to, m_to = pairs_of(k, m)
            pairs.append((k * mu + m, (k_to % ka) * mu + m_to % mu))
    return lax.ppermute(value, ("ka", "mu"), pairs)


def target_of(slot, k):
    sign = 1 - 2 * (k % 2)
    return k + sign * {NEAR: 1, FAR: -1, AHEAD: 2, BEHIND: -2}[slot]


def local(vectors, phi_val, phi_con, screened, partner):
    del partner
    ka, count = lax.axis_size("ka"), lax.axis_size("mu")
    vec_count, local_k, local_pairs = vectors.shape
    _, valence, rows_m = phi_val.shape
    _, conduction, _ = phi_con.shape
    points = screened.shape[2]
    if local_k != 1 or ka % 2:
        raise ValueError("unsupported shapes")
    rows = local_pairs // conduction

    me, parity = lax.axis_index("mu"), lax.axis_index("ka") % 2
    info = jnp.concatenate([me[None], jnp.arange(4) ^ parity]).astype(jnp.int32)

    def from_slot(slot):
        back = {NEAR: NEAR, FAR: FAR, AHEAD: BEHIND, BEHIND: AHEAD}[slot]
        if slot in (AHEAD, BEHIND):
            return lambda k, m: (target_of(back, k), m)
        return lambda k, m: (target_of(slot, k), m)

    def over_mu(value):
        return [value] + [moved(value, lambda k, m, t=t: (k, m - t)) for t in range(1, count)]

    con_home = phi_con[0]
    vec_home = vectors.astype(BF16).reshape(vec_count, rows, conduction)
    vec_home, con_home = lax.optimization_barrier((vec_home, con_home))
    bundle_home = jnp.concatenate([phi_val[0], con_home], axis=0)
    vec_parts = over_mu(vec_home)
    con_parts = over_mu(con_home)
    bundle = {s: moved(bundle_home, from_slot(s)) for s in (NEAR, AHEAD, BEHIND)}
    bundle[FAR] = moved(bundle[AHEAD], from_slot(NEAR))
    others = {s: over_mu(bundle[s][valence:])[1:] for s in (AHEAD, BEHIND)}
    others[NEAR] = [moved(part, from_slot(NEAR)) for part in con_parts[1:]]
    others[FAR] = [moved(part, from_slot(NEAR)) for part in others[AHEAD]]

    pairs_type = jax.ShapeDtypeStruct((vec_count, rows_m, points), BF16)
    folded_type = jax.ShapeDtypeStruct((vec_count * valence, points), BF16)
    weight_type = jax.ShapeDtypeStruct((rows_m, points), BF16)
    fold_flops = 2 * vec_count * valence * rows_m * points

    def params(mib):
        return pltpu.CompilerParams(vmem_limit_bytes=mib * MIB)

    later = (AHEAD, BEHIND)
    first = pl.pallas_call(
        functools.partial(first_kernel, count, later),
        out_shape=[pairs_type, folded_type] + [weight_type] * len(later),
        in_specs=[SMEM_SPEC] + [VMEM_SPEC] * (2 * count + 1) + [HBM_SPEC],
        out_specs=[VMEM_SPEC] * (2 + len(later)),
        scratch_shapes=[
            pltpu.VMEM((vec_count, valence, conduction), F32),
            pltpu.VMEM((rows_m, points), BF16),
            pltpu.SemaphoreType.DMA((1 + len(later), count)),
        ],
        compiler_params=params(24),
        cost_estimate=pl.CostEstimate(flops=8 * fold_flops, bytes_accessed=4 * MIB, transcendentals=0),
        name="first",
    )
    pairs, folded_near, *weights = first(
        info, *vec_parts, *con_parts[1:], bundle_home, bundle[NEAR], screened
    )

    def fold(pairs, weights, slots, later):
        used = len(slots)
        extra = len(later)
        out = pl.pallas_call(
            functools.partial(fold_kernel, count, used, later),
            out_shape=[pairs_type] * bool(extra)
            + [folded_type] * used
            + [weight_type] * extra,
            in_specs=[SMEM_SPEC]
            + [VMEM_SPEC] * (1 + 2 * used)
            + [HBM_SPEC] * bool(extra),
            out_specs=[VMEM_SPEC] * (bool(extra) + used + extra),
            scratch_shapes=[pltpu.SemaphoreType.DMA((extra, count))] * bool(extra),
            input_output_aliases={1: 0} if extra else {},
            compiler_params=params(20),
            cost_estimate=pl.CostEstimate(
                flops=4 * used * fold_flops, bytes_accessed=4 * used * MIB, transcendentals=0
            ),
        )(info, pairs, *[bundle[s] for s in slots], *weights, *[screened] * bool(extra))
        if extra:
            pairs, out = out[0], out[1:]
        return pairs, out[:used], out[used:]

    pairs, (folded_ahead, folded_behind), weights = fold(pairs, weights, (AHEAD, BEHIND), (FAR,))
    _, (folded_far,), _ = fold(pairs, weights, (FAR,), ())

    result = (count, vec_count, rows, conduction)
    order = (NEAR, FAR, AHEAD, BEHIND)
    near, far, behind = pl.pallas_call(
        functools.partial(result_kernel, count),
        out_shape=[jax.ShapeDtypeStruct(s, F32) for s in ((2,) + result, result, result)],
        in_specs=[SMEM_SPEC] + [VMEM_SPEC] * (4 + 4 * count),
        out_specs=[VMEM_SPEC] * 3,
        scratch_shapes=[pltpu.VMEM((4, vec_count * valence, conduction), F32)],
        compiler_params=params(10),
        cost_estimate=pl.CostEstimate(flops=fold_flops, bytes_accessed=MIB, transcendentals=0),
        name="result",
    )(
        info,
        folded_near,
        folded_far,
        folded_ahead,
        folded_behind,
        *[bundle[s] for s in order],
        *[part for s in order for part in others[s]],
    )
    near = moved(near, lambda k, m: (target_of(NEAR, k), m))
    shared = jnp.stack([near[0], far + near[1], behind])
    summed = shared[:, 0]
    for part in range(1, count):
        sent = shared[:, part].astype(BF16)
        summed += moved(sent, lambda k, m, part=part: (k, m + part)).astype(F32)
    arrived = moved(summed[1:].astype(BF16), lambda k, m: (target_of(BEHIND, k), m))
    from_near = moved(arrived[0], lambda k, m: (target_of(NEAR, k), m))
    total = summed[0] + arrived[1].astype(F32) + from_near.astype(F32)
    return total.reshape(vec_count, 1, local_pairs)


def solution(mesh):
    placed = (
        P(None, "ka", "mu"),
        P("ka", None, "mu"),
        P("ka", None, "mu"),
        P(None, "mu", None),
        P("ka", None),
    )

    return jax.shard_map(
        local, mesh=mesh, in_specs=placed, out_specs=P(None, "ka", "mu"), check_vma=False
    )
```

```python
import functools

import jax
import jax.numpy as jnp
from jax import lax
from jax.experimental import pallas as pl
from jax.experimental.pallas import tpu as pltpu
from jax.sharding import PartitionSpec as P

BF16, F32 = jnp.bfloat16, jnp.float32
VMEM_SPEC = pl.BlockSpec(memory_space=pltpu.VMEM)
SMEM_SPEC = pl.BlockSpec(memory_space=pltpu.SMEM)
HBM_SPEC = pl.BlockSpec(memory_space=pltpu.HBM)
MIB = 1 << 20
NEAR, FAR, AHEAD, BEHIND = range(4)


def contract(left, right, left_dim, right_dim):
    dims = (((left_dim,), (right_dim,)), ((), ()))
    return lax.dot_general(left, right, dims, preferred_element_type=F32)


def screened_copy(screened, info, slot, part, cols, buffer, sem):
    count = screened.shape[2] // cols
    home = lax.rem(info[0] + part, count)
    columns = pl.ds(pl.multiple_of(home * cols, cols), cols)
    return pltpu.make_async_copy(
        screened.at[info[1 + slot], :, columns], buffer.at[:, pl.ds(part * cols, cols)], sem
    )


def first_kernel(count, later, info, *refs):
    vec_parts, con_others = refs[:count], refs[count : 2 * count - 1]
    bundle_home, bundle_near, screened = refs[2 * count - 1 : 2 * count + 2]
    pairs, folded = refs[2 * count + 2 : 2 * count + 4]
    weights = refs[2 * count + 4 : -3]
    vec_all, buffer, sems = refs[-3:]
    vec_count, rows, _ = vec_parts[0].shape
    cols = bundle_home.shape[1]
    _, valence, conduction = vec_all.shape
    slots, buffers = (NEAR,) + later, (buffer,) + tuple(weights)

    def copies(i):
        return [
            screened_copy(screened, info, slots[i], part, cols, buffers[i], sems.at[i, part])
            for part in range(count)
        ]

    for i in range(len(slots)):
        for copy in copies(i):
            copy.start()
    for part in range(count):
        offset = pl.multiple_of(lax.rem(info[0] + part, count) * rows, rows)
        for s in range(vec_count):
            vec_all[s, pl.ds(offset, rows), :] = vec_parts[part][s].astype(F32)
    val_points = jnp.transpose(bundle_home[pl.ds(0, valence), :])
    for s in range(vec_count):
        vec = vec_all[s].astype(BF16)
        for part in range(count):
            con = con_others[part - 1][...] if part else bundle_home[pl.ds(valence, conduction), :]
            blended = contract(vec, con, 1, 0).astype(BF16)
            pairs[s, :, pl.ds(part * cols, cols)] = contract(val_points, blended, 1, 0).astype(BF16)
    for copy in copies(0):
        copy.wait()
    for s in range(vec_count):
        folded[pl.ds(s * valence, valence), :] = contract(
            bundle_near[pl.ds(0, valence), :], buffer[...] * pairs[s], 1, 0
        ).astype(BF16)
    for i in range(1, len(slots)):
        for copy in copies(i):
            copy.wait()


def fold_kernel(count, used, later, info, *refs):
    pairs = refs[0]
    bundles, weights = refs[1 : 1 + used], refs[1 + used : 1 + 2 * used]
    outs = refs[1 + 2 * used :]
    if later:
        screened, outs = outs[0], outs[2:-1]
    foldeds, nexts = outs[:used], outs[used:]
    vec_count, _, points = pairs.shape
    cols = points // count
    valence = foldeds[0].shape[0] // vec_count

    def copies(i):
        return [
            screened_copy(screened, info, later[i], part, cols, nexts[i], refs[-1].at[i, part])
            for part in range(count)
        ]

    for i in range(len(later)):
        for copy in copies(i):
            copy.start()
    for i in range(used):
        for s in range(vec_count):
            foldeds[i][pl.ds(s * valence, valence), :] = contract(
                bundles[i][pl.ds(0, valence), :], weights[i][...] * pairs[s], 1, 0
            ).astype(BF16)
    for i in range(len(later)):
        for copy in copies(i):
            copy.wait()


def result_kernel(count, used, info, *refs):
    foldeds, bundles = refs[:used], refs[used : 2 * used]
    others = refs[2 * used : 2 * used + used * (count - 1)]
    arrays, work = refs[2 * used + used * (count - 1) : -1], refs[-1]
    outs = [array.at[i] for array in arrays for i in range(array.shape[0])]
    _, _, vec_count, rows, _ = arrays[0].shape
    valence = foldeds[0].shape[0] // vec_count
    cols = bundles[0].shape[1]
    for i in range(used):
        total = contract(
            foldeds[i][:, pl.ds(0, cols)], bundles[i][pl.ds(valence, bundles[i].shape[0] - valence), :], 1, 1
        )
        for part in range(1, count):
            total += contract(
                foldeds[i][:, pl.ds(part * cols, cols)],
                others[i * (count - 1) + part - 1][...],
                1,
                1,
            )
        work[i] = total
        for part in range(count):
            offset = lax.rem(info[0] + part, count) * rows
            for s in range(vec_count):
                start = pl.multiple_of(s * valence + offset, 8)
                outs[i][part, s] = work[i, pl.ds(start, rows), :]


def moved(value, pairs_of):
    ka, mu = lax.axis_size("ka"), lax.axis_size("mu")
    pairs = []
    for k in range(ka):
        for m in range(mu):
            k_to, m_to = pairs_of(k, m)
            pairs.append((k * mu + m, (k_to % ka) * mu + m_to % mu))
    return lax.ppermute(value, ("ka", "mu"), pairs)


def target_of(slot, k):
    sign = 1 - 2 * (k % 2)
    return k + sign * {NEAR: 1, FAR: -1, AHEAD: 2, BEHIND: -2}[slot]


def local(vectors, phi_val, phi_con, screened, partner):
    del partner
    ka, count = lax.axis_size("ka"), lax.axis_size("mu")
    vec_count, local_k, local_pairs = vectors.shape
    _, valence, rows_m = phi_val.shape
    _, conduction, _ = phi_con.shape
    points = screened.shape[2]
    if local_k != 1 or ka % 2:
        raise ValueError("unsupported shapes")
    rows = local_pairs // conduction

    me, parity = lax.axis_index("mu"), lax.axis_index("ka") % 2
    info = jnp.concatenate([me[None], jnp.arange(4) ^ parity]).astype(jnp.int32)

    def from_slot(slot):
        back = {NEAR: NEAR, FAR: FAR, AHEAD: BEHIND, BEHIND: AHEAD}[slot]
        if slot in (AHEAD, BEHIND):
            return lambda k, m: (target_of(back, k), m)
        return lambda k, m: (target_of(slot, k), m)

    def over_mu(value):
        return [value] + [moved(value, lambda k, m, t=t: (k, m - t)) for t in range(1, count)]

    con_home = phi_con[0]
    vec_home = vectors.astype(BF16).reshape(vec_count, rows, conduction)
    vec_home, con_home = lax.optimization_barrier((vec_home, con_home))
    bundle_home = jnp.concatenate([phi_val[0], con_home], axis=0)
    vec_parts = over_mu(vec_home)
    con_parts = over_mu(con_home)
    bundle = {s: moved(bundle_home, from_slot(s)) for s in (NEAR, AHEAD, BEHIND)}
    bundle[FAR] = moved(bundle[AHEAD], from_slot(NEAR))
    others = {s: over_mu(bundle[s][valence:])[1:] for s in (AHEAD, BEHIND)}
    others[NEAR] = [moved(part, from_slot(NEAR)) for part in con_parts[1:]]
    others[FAR] = [moved(part, from_slot(NEAR)) for part in others[AHEAD]]

    pairs_type = jax.ShapeDtypeStruct((vec_count, rows_m, points), BF16)
    folded_type = jax.ShapeDtypeStruct((vec_count * valence, points), BF16)
    weight_type = jax.ShapeDtypeStruct((rows_m, points), BF16)
    fold_flops = 2 * vec_count * valence * rows_m * points

    def params(mib):
        return pltpu.CompilerParams(vmem_limit_bytes=mib * MIB)

    later = (AHEAD, BEHIND)
    first = pl.pallas_call(
        functools.partial(first_kernel, count, later),
        out_shape=[pairs_type, folded_type] + [weight_type] * len(later),
        in_specs=[SMEM_SPEC] + [VMEM_SPEC] * (2 * count + 1) + [HBM_SPEC],
        out_specs=[VMEM_SPEC] * (2 + len(later)),
        scratch_shapes=[
            pltpu.VMEM((vec_count, valence, conduction), F32),
            pltpu.VMEM((rows_m, points), BF16),
            pltpu.SemaphoreType.DMA((1 + len(later), count)),
        ],
        compiler_params=params(24),
        cost_estimate=pl.CostEstimate(flops=8 * fold_flops, bytes_accessed=4 * MIB, transcendentals=0),
        name="first",
    )
    pairs, folded_near, *weights = first(
        info, *vec_parts, *con_parts[1:], bundle_home, bundle[NEAR], screened
    )

    def fold(pairs, weights, slots, later):
        used = len(slots)
        extra = len(later)
        out = pl.pallas_call(
            functools.partial(fold_kernel, count, used, later),
            out_shape=[pairs_type] * bool(extra)
            + [folded_type] * used
            + [weight_type] * extra,
            in_specs=[SMEM_SPEC]
            + [VMEM_SPEC] * (1 + 2 * used)
            + [HBM_SPEC] * bool(extra),
            out_specs=[VMEM_SPEC] * (bool(extra) + used + extra),
            scratch_shapes=[pltpu.SemaphoreType.DMA((extra, count))] * bool(extra),
            input_output_aliases={1: 0} if extra else {},
            compiler_params=params(20),
            cost_estimate=pl.CostEstimate(
                flops=4 * used * fold_flops, bytes_accessed=4 * used * MIB, transcendentals=0
            ),
        )(info, pairs, *[bundle[s] for s in slots], *weights, *[screened] * bool(extra))
        if extra:
            pairs, out = out[0], out[1:]
        return pairs, out[:used], out[used:]

    pairs, (folded_ahead, folded_behind), weights = fold(pairs, weights, (AHEAD, BEHIND), (FAR,))

    def results(foldeds, slots, groups):
        used = len(slots)
        return pl.pallas_call(
            functools.partial(result_kernel, count, used),
            out_shape=[
                jax.ShapeDtypeStruct((n, count, vec_count, rows, conduction), F32)
                for n in groups
            ],
            in_specs=[SMEM_SPEC] + [VMEM_SPEC] * (used + used * count),
            out_specs=[VMEM_SPEC] * len(groups),
            scratch_shapes=[pltpu.VMEM((used, vec_count * valence, conduction), F32)],
            compiler_params=params(10),
            cost_estimate=pl.CostEstimate(
                flops=used * fold_flops // 4, bytes_accessed=MIB, transcendentals=0
            ),
        )(
            info,
            *foldeds,
            *[bundle[slot] for slot in slots],
            *[part for slot in slots for part in others[slot]],
        )

    early = (folded_near, folded_ahead, folded_behind)
    near, behind = results(early, (NEAR, AHEAD, BEHIND), (2, 1))
    near = moved(near, lambda k, m: (target_of(NEAR, k), m))
    _, (folded_far,), _ = fold(pairs, weights, (FAR,), ())
    (far,) = results((folded_far,), (FAR,), (1,))
    shared = jnp.stack([near[0], far[0] + near[1], behind[0]])
    summed = shared[:, 0]
    for part in range(1, count):
        sent = shared[:, part].astype(BF16)
        summed += moved(sent, lambda k, m, part=part: (k, m + part)).astype(F32)
    arrived = moved(summed[1:].astype(BF16), lambda k, m: (target_of(BEHIND, k), m))
    from_near = moved(arrived[0], lambda k, m: (target_of(NEAR, k), m))
    total = summed[0] + arrived[1].astype(F32) + from_near.astype(F32)
    return total.reshape(vec_count, 1, local_pairs)


def solution(mesh):
    placed = (
        P(None, "ka", "mu"),
        P("ka", None, "mu"),
        P("ka", None, "mu"),
        P(None, "mu", None),
        P("ka", None),
    )

    return jax.shard_map(
        local, mesh=mesh, in_specs=placed, out_specs=P(None, "ka", "mu"), check_vma=False
    )
```
